32 devices in a mesh: tensor: 2 (over y), context: 16 (over z, x, core).
Axes of the slice: x: 2, y: 2, z: 4, core: 2. Of those that a mesh axis runs over, the one named last changes fastest.
Arguments:
- hidden_in: bfloat16 [8192, 4096], P('context', 'tensor'), may hold values from -6 to 6
- norm_gain: bfloat16 [4096], replicated, may hold values from 0.099609375 to 1.8984375
- w_query: bfloat16 [4096, 4096], P('context', 'tensor'), may hold values from -0.09375 to 0.09375
- w_key: bfloat16 [4096, 1024], P('context', 'tensor'), may hold values from -0.09375 to 0.09375
- w_value: bfloat16 [4096, 1024], P('context', 'tensor'), may hold values from -0.09375 to 0.09375
- kv_cache: bfloat16 [16384, 2, 1024], P('context', None, 'tensor'), may hold values from -68 to 68
- selected: int32 [16, 3], replicated, may hold values from 0 to 127, as said below
Outputs:
- attended: bfloat16 [8192, 4096], P('context', 'tensor')
The draws below stay inside these ranges and needn't reach their ends.
Inputs may be any that keep to these rules, and one draw needn't show every extreme that they name: `selected`: each row names 3 cache blocks held by 3 different devices of context (block c is held by device c // 8). The blocks held by one device are named at most 6 times over all rows together, and those of one device exactly 6 times.
All inputs are finite; a program needn't handle non-finite values.
Results may differ from the reference program's by a relative error of at most 0.011.
The reference program's roundings to bfloat16 on the way (of `normed`, `query` and `probs`) count: a program that leaves them out, or rounds other values in their place, can miss the bound.
Values may be sent and summed in bfloat16 or wider, within the bound.
A program may use at most 128 MiB of HBM per device.

```python
import math
import jax
import jax.numpy as jnp
from jax import lax

D = 4096
HEADS = 32
KV_HEADS = 8
HEAD_DIM = 128
Q_BLOCK = 512
C_BLOCK = 128
PICKS = 3
MOST_REQ = 6
BLOCKS_DEV = 8
TOKENS = 8192
CACHE_BLOCKS = 128
CACHE_TOKENS = 16384
N_CONTEXT = 16


def draw_kv_cache(key, part):
    first_key = jax.random.fold_in(key, 0)
    array_shape = (CACHE_BLOCKS, C_BLOCK, 2, KV_HEADS, HEAD_DIM)
    values = jnp.clip(jax.random.normal(first_key, array_shape, jnp.float32), -4.0, 4.0)
    return values.reshape(CACHE_TOKENS, 2, KV_HEADS * HEAD_DIM).astype(jnp.bfloat16)


def draw_selected(key, part):
    devices = N_CONTEXT
    key_hot, key_order, key_offset, key_rows = jax.random.split(key, 4)
    hottest = jax.random.randint(key_hot, (), 0, devices)
    others = jax.random.permutation(key_order, devices - 1)
    others = others + (others >= hottest).astype(jnp.int32)
    serial = jnp.arange(devices * PICKS, dtype=jnp.int32).reshape(PICKS, devices)
    spot = jnp.mod(serial - MOST_REQ, devices - 1)
    holder = jnp.where(serial < MOST_REQ, hottest, others[spot])
    offset = jax.random.randint(key_offset, (PICKS, devices), 0, BLOCKS_DEV)
    shuffle = jax.random.permutation(key_rows, devices)
    numbers = (holder * BLOCKS_DEV + offset)[:, shuffle]
    return numbers.T.astype(jnp.int32)


def shard_levels(rng, shape, shards, low, top_value):
    level = 1.0
    for axis_at, parts in shards:
        draws = jax.random.uniform(jax.random.fold_in(jax.random.fold_in(rng, 6), axis_at), (parts,), jnp.float32, low / len(shards), top_value / len(shards))
        level = level * jnp.repeat(jnp.exp(draws), shape[axis_at] // parts).reshape((-1,) + (1,) * (len(shape) - 1 - axis_at))
    return level


def bell_draw(key, dims, scale, reach, pieces=(), held_as=jnp.bfloat16):
    factor_of = shard_levels(key, dims, pieces, -0.22, 0.18) if pieces else 1.0
    drawn = jax.random.normal(key, dims, jnp.float32) * scale * factor_of
    return jnp.minimum(jnp.maximum(drawn, -reach), reach).astype(held_as)


def setup_inputs(seed: int = 0) -> dict:
    key_list = jax.random.split(jax.random.key(seed), 8)
    hidden_in = bell_draw(key_list[0], (TOKENS, D), 1.0, 6.0, ((0, 16), (1, 2)))
    norm_gain = jnp.clip(1.0 + 0.18 * jax.random.normal(key_list[1], (D,), jnp.float32), 0.099609375, 1.8984375).astype(jnp.bfloat16)
    w_query = bell_draw(key_list[2], (D, HEADS * HEAD_DIM), D ** -0.5, 0.09375, ((0, 16), (1, 2)))
    w_key = bell_draw(key_list[3], (D, KV_HEADS * HEAD_DIM), D ** -0.5, 0.09375, ((0, 16), (1, 2)))
    w_value = bell_draw(key_list[4], (D, KV_HEADS * HEAD_DIM), D ** -0.5, 0.09375, ((0, 16), (1, 2)))
    kv_cache = draw_kv_cache(jax.random.fold_in(key_list[7], 71), 0)
    selected = draw_selected(jax.random.fold_in(key_list[7], 71), 0)
    return {"hidden_in": hidden_in, "norm_gain": norm_gain, "w_query": w_query, "w_key": w_key, "w_value": w_value, "kv_cache": kv_cache, "selected": selected}


def reference(hidden_in, norm_gain, w_query, w_key, w_value, kv_cache, selected):
    floats = hidden_in.astype(jnp.float32)
    inverse_rms = lax.rsqrt(lax.optimization_barrier(jnp.mean(floats * floats, axis=1, keepdims=True)) + 1e-05)
    normed = (floats * inverse_rms * norm_gain.astype(jnp.float32)).astype(jnp.bfloat16)
    query = jnp.dot(normed, w_query, preferred_element_type=jnp.float32).astype(jnp.bfloat16)
    fresh_key = jnp.dot(normed, w_key, preferred_element_type=jnp.float32).astype(jnp.bfloat16)
    fresh_value = jnp.dot(normed, w_value, preferred_element_type=jnp.float32).astype(jnp.bfloat16)
    groups = HEADS // KV_HEADS
    blocks = kv_cache.reshape(CACHE_BLOCKS, C_BLOCK, 2, KV_HEADS, HEAD_DIM)
    cached = PICKS * C_BLOCK
    score_scale = 1.0 / math.sqrt(HEAD_DIM)
    row_index = jnp.arange(Q_BLOCK, dtype=jnp.int32)[:, None]
    col_index = jnp.arange(cached + Q_BLOCK, dtype=jnp.int32)[None, :]
    visible = (col_index < cached) | (col_index - cached <= row_index)

    def one_block(block_number):
        start = block_number * Q_BLOCK
        query_rows = lax.dynamic_slice_in_dim(query, start, Q_BLOCK, 0).reshape(Q_BLOCK, KV_HEADS, groups, HEAD_DIM)
        key_rows = lax.dynamic_slice_in_dim(fresh_key, start, Q_BLOCK, 0).reshape(Q_BLOCK, KV_HEADS, HEAD_DIM)
        value_rows = lax.dynamic_slice_in_dim(fresh_value, start, Q_BLOCK, 0).reshape(Q_BLOCK, KV_HEADS, HEAD_DIM)
        chosen = jnp.take(blocks, selected[block_number], axis=0)
        keys_all = jnp.concatenate([chosen[:, :, 0].reshape(cached, KV_HEADS, HEAD_DIM), key_rows], axis=0)
        values_all = jnp.concatenate([chosen[:, :, 1].reshape(cached, KV_HEADS, HEAD_DIM), value_rows], axis=0)
        scores = jnp.einsum('qhgd,khd->hgqk', query_rows.astype(jnp.float32), keys_all.astype(jnp.float32)) * score_scale
        scores = jnp.where(visible[None, None], scores, -jnp.inf)
        probs = jax.nn.softmax(scores, axis=-1).astype(jnp.bfloat16)
        output = jnp.einsum('hgqk,khd->qhgd', probs.astype(jnp.float32), values_all.astype(jnp.float32))
        return output.astype(jnp.bfloat16).reshape(Q_BLOCK, HEADS * HEAD_DIM)
    results = lax.map(one_block, jnp.arange(N_CONTEXT, dtype=jnp.int32))
    return results.reshape(TOKENS, HEADS * HEAD_DIM)
```

```python
import math

import jax
import jax.numpy as jnp
from jax import lax
from jax.experimental import pallas as pl
from jax.experimental.pallas import tpu as pltpu
from jax.sharding import PartitionSpec as P

HEAD_DIM = 128
C_BLOCK = 128
PICKS = 3
MOST_REQ = 6
BLOCKS_DEV = 8
ROW_TILE = 256


def attend_kernel(q_ref, k_ref, v_ref, ck_ref, cv_ref, *rest):
    o_ref = rest[-1]
    rows = q_ref.shape[0]
    scale = 1.0 / math.sqrt(HEAD_DIM)
    dims = (((1,), (1,)), ((), ()))
    for start in range(0, rows, ROW_TILE):
        stop = start + ROW_TILE
        query = q_ref[start:stop, :]
        cached = lax.dot_general(query, ck_ref[...], dims, preferred_element_type=jnp.float32) * scale
        fresh = lax.dot_general(query, k_ref[:stop, :], dims, preferred_element_type=jnp.float32) * scale
        row = lax.broadcasted_iota(jnp.int32, fresh.shape, 0) + start
        col = lax.broadcasted_iota(jnp.int32, fresh.shape, 1)
        fresh = jnp.where(col <= row, fresh, -jnp.inf)
        top = jnp.maximum(jnp.max(cached, axis=1, keepdims=True), jnp.max(fresh, axis=1, keepdims=True))
        cached = jnp.exp(cached - top)
        fresh = jnp.exp(fresh - top)
        total = jnp.sum(cached, axis=1, keepdims=True) + jnp.sum(fresh, axis=1, keepdims=True)
        inverse = 1.0 / total
        mixed = jnp.dot(
            (cached * inverse).astype(jnp.bfloat16), cv_ref[...], preferred_element_type=jnp.float32
        )
        mixed += jnp.dot(
            (fresh * inverse).astype(jnp.bfloat16), v_ref[:stop, :], preferred_element_type=jnp.float32
        )
        o_ref[start:stop, :] = mixed.astype(o_ref.dtype)


def attend(projected, cached_key, cached_value, earlier, group, groups, local_heads):
    rows = projected.shape[0]
    cached = cached_key.shape[0]
    column = lambda place: pl.BlockSpec((rows, HEAD_DIM), lambda h: (0, place))
    operands = [projected, projected, projected, cached_key, cached_value]
    specs = [
        pl.BlockSpec((rows, HEAD_DIM), lambda h: (0, h)),
        column(groups),
        column(groups + 1),
        pl.BlockSpec((cached, HEAD_DIM), lambda h: (0, group)),
        pl.BlockSpec((cached, HEAD_DIM), lambda h: (0, group)),
    ]
    aliases = {}
    if earlier is not None:
        operands.append(earlier)
        specs.append(pl.BlockSpec(memory_space=pl.ANY))
        aliases = {5: 0}
    return pl.pallas_call(
        attend_kernel,
        grid=(groups,),
        out_shape=jax.ShapeDtypeStruct((rows, local_heads * groups * HEAD_DIM), jnp.bfloat16),
        in_specs=specs,
        out_specs=pl.BlockSpec((rows, HEAD_DIM), lambda h: (0, group * groups + h)),
        input_output_aliases=aliases,
        cost_estimate=pl.CostEstimate(
            flops=4 * groups * rows * (cached + rows) * HEAD_DIM,
            bytes_accessed=4 * groups * rows * HEAD_DIM,
            transcendentals=groups * rows * (cached + rows),
        ),
        compiler_params=pltpu.CompilerParams(vmem_limit_bytes=24 << 20),
        name="attend",
    )(*operands)


def fetch_blocks(kv_cache, selected):
    local_heads = kv_cache.shape[2] // HEAD_DIM
    devices = lax.axis_size("context")
    myself = lax.axis_index("context")
    owners = selected // BLOCKS_DEV
    offsets = selected % BLOCKS_DEV
    blocks = kv_cache.reshape(BLOCKS_DEV, C_BLOCK, 2, local_heads, HEAD_DIM)
    listings = devices * PICKS
    piece_rows = C_BLOCK // devices
    flat_owner = owners.reshape(listings)
    flat_offset = offsets.reshape(listings)
    serial = jnp.arange(listings, dtype=jnp.int32)
    earlier = (flat_owner[:, None] == flat_owner[None, :]) & (serial[:, None] > serial[None, :])
    ranks = jnp.sum(earlier.astype(jnp.int32), axis=1)
    slots = jnp.arange(MOST_REQ, dtype=jnp.int32)
    hits = (flat_owner[None, :] == myself) & (ranks[None, :] == slots[:, None])
    filled = jnp.any(hits, axis=1)
    picked = jnp.sum(jnp.where(hits, flat_offset[None, :], 0), axis=1)
    outbox = jnp.where(
        filled[:, None, None, None, None],
        jnp.take(blocks, picked, axis=0),
        jnp.zeros((), jnp.bfloat16),
    )
    outbox = outbox.reshape(MOST_REQ, devices, piece_rows, 2, local_heads, HEAD_DIM)
    spread = lax.all_to_all(outbox, "context", split_axis=1, concat_axis=1, tiled=True)
    relayed = spread.reshape(MOST_REQ * devices, piece_rows, 2, local_heads, HEAD_DIM)
    forward = jnp.take(relayed, ranks * devices + flat_owner, axis=0)
    forward = forward.reshape(devices, PICKS, piece_rows, 2, local_heads, HEAD_DIM)
    collected = lax.all_to_all(forward, "context", split_axis=0, concat_axis=2, tiled=True)
    fetched = collected[0]
    cached = fetched.shape[0] * fetched.shape[1]
    cached_key = fetched[:, :, 0].reshape(cached, local_heads * HEAD_DIM)
    cached_value = fetched[:, :, 1].reshape(cached, local_heads * HEAD_DIM)
    return cached_key, cached_value


def gather_features(hidden_in):
    if lax.axis_size("tensor") != 2:
        return lax.all_gather(hidden_in, "tensor", axis=1, tiled=True)
    other = lax.ppermute(hidden_in, "tensor", [(0, 1), (1, 0)])
    first = lax.axis_index("tensor") == 0
    return jnp.concatenate(
        [jnp.where(first, hidden_in, other), jnp.where(first, other, hidden_in)], axis=1
    )


def on_device(hidden_in, norm_gain, w_query, w_key, w_value, kv_cache, selected):
    local_heads = kv_cache.shape[2] // HEAD_DIM
    groups = w_query.shape[1] // (HEAD_DIM * local_heads)
    span = groups * HEAD_DIM
    weights = []
    for g in range(local_heads):
        stacked = jnp.concatenate(
            [
                w_query[:, g * span : (g + 1) * span],
                w_key[:, g * HEAD_DIM : (g + 1) * HEAD_DIM],
                w_value[:, g * HEAD_DIM : (g + 1) * HEAD_DIM],
            ],
            axis=1,
        )
        weights.append(lax.all_gather(stacked, "context", axis=0, tiled=True))
    gathered = gather_features(hidden_in)
    floats = gathered.astype(jnp.float32)
    inverse_rms = lax.rsqrt(jnp.mean(floats * floats, axis=1, keepdims=True) + 1e-05)
    normed = (floats * inverse_rms * norm_gain.astype(jnp.float32)).astype(jnp.bfloat16)
    normed = lax.optimization_barrier(normed)
    cached_key, cached_value = fetch_blocks(kv_cache, selected)
    result = None
    for g in range(local_heads):
        projected = jnp.dot(normed, weights[g], preferred_element_type=jnp.float32).astype(jnp.bfloat16)
        result = attend(projected, cached_key, cached_value, result, g, groups, local_heads)
    return result


def solution(mesh):
    return jax.shard_map(
        on_device,
        mesh=mesh,
        in_specs=(
            P("context", "tensor"),
            P(),
            P("context", "tensor"),
            P("context", "tensor"),
            P("context", "tensor"),
            P("context", None, "tensor"),
            P(),
        ),
        out_specs=P("context", "tensor"),
        check_vma=False,
    )
```

```python
import math

import jax
import jax.numpy as jnp
from jax import lax
from jax.experimental import pallas as pl
from jax.experimental.pallas import tpu as pltpu
from jax.sharding import PartitionSpec as P

HEAD_DIM = 128
C_BLOCK = 128
PICKS = 3
MOST_REQ = 6
BLOCKS_DEV = 8
ROW_TILE = 256


def attend_kernel(q_ref, k_ref, v_ref, ck_ref, cv_ref, *rest):
    o_ref = rest[-1]
    rows = q_ref.shape[0]
    scale = 1.0 / math.sqrt(HEAD_DIM)
    dims = (((1,), (1,)), ((), ()))
    for start in range(0, rows, ROW_TILE):
        stop = start + ROW_TILE
        query = q_ref[start:stop, :]
        cached = lax.dot_general(query, ck_ref[...], dims, preferred_element_type=jnp.float32) * scale
        fresh = lax.dot_general(query, k_ref[:stop, :], dims, preferred_element_type=jnp.float32) * scale
        row = lax.broadcasted_iota(jnp.int32, fresh.shape, 0) + start
        col = lax.broadcasted_iota(jnp.int32, fresh.shape, 1)
        fresh = jnp.where(col <= row, fresh, -jnp.inf)
        top = jnp.maximum(jnp.max(cached, axis=1, keepdims=True), jnp.max(fresh, axis=1, keepdims=True))
        cached = jnp.exp(cached - top)
        fresh = jnp.exp(fresh - top)
        total = jnp.sum(cached, axis=1, keepdims=True) + jnp.sum(fresh, axis=1, keepdims=True)
        inverse = 1.0 / total
        mixed = jnp.dot(
            (cached * inverse).astype(jnp.bfloat16), cv_ref[...], preferred_element_type=jnp.float32
        )
        mixed += jnp.dot(
            (fresh * inverse).astype(jnp.bfloat16), v_ref[:stop, :], preferred_element_type=jnp.float32
        )
        o_ref[start:stop, :] = mixed.astype(o_ref.dtype)


def attend(projected, cached_key, cached_value, groups, local_heads):
    rows = projected.shape[0]
    cached = cached_key.shape[0]
    heads = groups * local_heads
    tall = lambda height, place: pl.BlockSpec((height, HEAD_DIM), lambda h: (0, place(h)))
    return pl.pallas_call(
        attend_kernel,
        grid=(heads,),
        out_shape=jax.ShapeDtypeStruct((rows, heads * HEAD_DIM), jnp.bfloat16),
        in_specs=[
            tall(rows, lambda h: h),
            tall(rows, lambda h: heads + h // groups),
            tall(rows, lambda h: heads + local_heads + h // groups),
            tall(cached, lambda h: h // groups),
            tall(cached, lambda h: h // groups),
        ],
        out_specs=tall(rows, lambda h: h),
        cost_estimate=pl.CostEstimate(
            flops=4 * heads * rows * (cached + rows) * HEAD_DIM,
            bytes_accessed=4 * heads * rows * HEAD_DIM,
            transcendentals=heads * rows * (cached + rows),
        ),
        compiler_params=pltpu.CompilerParams(vmem_limit_bytes=24 << 20),
        name="attend",
    )(projected, projected, projected, cached_key, cached_value)


def fetch_blocks(kv_cache, selected):
    local_heads = kv_cache.shape[2] // HEAD_DIM
    devices = lax.axis_size("context")
    myself = lax.axis_index("context")
    owners = selected // BLOCKS_DEV
    offsets = selected % BLOCKS_DEV
    blocks = kv_cache.reshape(BLOCKS_DEV, C_BLOCK, 2, local_heads, HEAD_DIM)
    listings = devices * PICKS
    piece_rows = C_BLOCK // devices
    flat_owner = owners.reshape(listings)
    flat_offset = offsets.reshape(listings)
    serial = jnp.arange(listings, dtype=jnp.int32)
    earlier = (flat_owner[:, None] == flat_owner[None, :]) & (serial[:, None] > serial[None, :])
    ranks = jnp.sum(earlier.astype(jnp.int32), axis=1)
    slots = jnp.arange(MOST_REQ, dtype=jnp.int32)
    hits = (flat_owner[None, :] == myself) & (ranks[None, :] == slots[:, None])
    filled = jnp.any(hits, axis=1)
    picked = jnp.sum(jnp.where(hits, flat_offset[None, :], 0), axis=1)
    outbox = jnp.where(
        filled[:, None, None, None, None],
        jnp.take(blocks, picked, axis=0),
        jnp.zeros((), jnp.bfloat16),
    )
    outbox = outbox.reshape(MOST_REQ, devices, piece_rows, 2, local_heads, HEAD_DIM)
    spread = lax.all_to_all(outbox, "context", split_axis=1, concat_axis=1, tiled=True)
    relayed = spread.reshape(MOST_REQ * devices, piece_rows, 2, local_heads, HEAD_DIM)
    forward = jnp.take(relayed, ranks * devices + flat_owner, axis=0)
    forward = forward.reshape(devices, PICKS, piece_rows, 2, local_heads, HEAD_DIM)
    collected = lax.all_to_all(forward, "context", split_axis=0, concat_axis=2, tiled=True)
    fetched = collected[0]
    cached = fetched.shape[0] * fetched.shape[1]
    cached_key = fetched[:, :, 0].reshape(cached, local_heads * HEAD_DIM)
    cached_value = fetched[:, :, 1].reshape(cached, local_heads * HEAD_DIM)
    return cached_key, cached_value


def gather_features(hidden_in):
    if lax.axis_size("tensor") != 2:
        return lax.all_gather(hidden_in, "tensor", axis=1, tiled=True)
    other = lax.ppermute(hidden_in, "tensor", [(0, 1), (1, 0)])
    first = lax.axis_index("tensor") == 0
    return jnp.concatenate(
        [jnp.where(first, hidden_in, other), jnp.where(first, other, hidden_in)], axis=1
    )


def on_device(hidden_in, norm_gain, w_query, w_key, w_value, kv_cache, selected):
    local_heads = kv_cache.shape[2] // HEAD_DIM
    groups = w_query.shape[1] // (HEAD_DIM * local_heads)
    stacked = jnp.concatenate([w_query, w_key, w_value], axis=1)
    weights = lax.all_gather(stacked, "context", axis=0, tiled=True)
    gathered = gather_features(hidden_in)
    floats = gathered.astype(jnp.float32)
    inverse_rms = lax.rsqrt(jnp.mean(floats * floats, axis=1, keepdims=True) + 1e-05)
    normed = (floats * inverse_rms * norm_gain.astype(jnp.float32)).astype(jnp.bfloat16)
    normed = lax.optimization_barrier(normed)
    cached_key, cached_value = fetch_blocks(kv_cache, selected)
    projected = jnp.dot(normed, weights, preferred_element_type=jnp.float32).astype(jnp.bfloat16)
    return attend(projected, cached_key, cached_value, groups, local_heads)


def solution(mesh):
    return jax.shard_map(
        on_device,
        mesh=mesh,
        in_specs=(
            P("context", "tensor"),
            P(),
            P("context", "tensor"),
            P("context", "tensor"),
            P("context", "tensor"),
            P("context", None, "tensor"),
            P(),
        ),
        out_specs=P("context", "tensor"),
        check_vma=False,
    )
```

```python
import functools
import math

import jax
import jax.numpy as jnp
from jax import lax
from jax.experimental import pallas as pl
from jax.experimental.pallas import tpu as pltpu
from jax.sharding import PartitionSpec as P

HEAD_DIM = 128
C_BLOCK = 128
PICKS = 3
MOST_REQ = 6
BLOCKS_DEV = 8
ROW_TILE = 256


def attend_kernel(groups, q_ref, k_ref, v_ref, ck_ref, cv_ref, o_ref):
    rows = q_ref.shape[0]
    tile = min(ROW_TILE, rows)
    factor = math.log2(math.e) / math.sqrt(HEAD_DIM)
    dims = (((1,), (1,)), ((), ()))
    for head in range(groups):
        place = slice(head * HEAD_DIM, (head + 1) * HEAD_DIM)
        for start in range(0, rows, tile):
            stop = start + tile
            query = q_ref[start:stop, place]
            cached = lax.dot_general(query, ck_ref[...], dims, preferred_element_type=jnp.float32)
            fresh = lax.dot_general(query, k_ref[:stop, :], dims, preferred_element_type=jnp.float32)
            row = lax.broadcasted_iota(jnp.int32, fresh.shape, 0) + start
            col = lax.broadcasted_iota(jnp.int32, fresh.shape, 1)
            fresh = jnp.where(col <= row, fresh, -jnp.inf)
            top = jnp.maximum(
                jnp.max(cached, axis=1, keepdims=True), jnp.max(fresh, axis=1, keepdims=True)
            )
            cached = jnp.exp2((cached - top) * factor)
            fresh = jnp.exp2((fresh - top) * factor)
            total = jnp.sum(cached, axis=1, keepdims=True) + jnp.sum(fresh, axis=1, keepdims=True)
            inverse = 1.0 / total
            mixed = jnp.dot(
                (cached * inverse).astype(jnp.bfloat16),
                cv_ref[...],
                preferred_element_type=jnp.float32,
            )
            mixed += jnp.dot(
                (fresh * inverse).astype(jnp.bfloat16),
                v_ref[:stop, :],
                preferred_element_type=jnp.float32,
            )
            o_ref[start:stop, place] = mixed.astype(o_ref.dtype)


def attend(projected, cached_key, cached_value, groups, local_heads):
    rows = projected.shape[0]
    cached = cached_key.shape[0]
    heads = groups * local_heads
    block = lambda height, width, place: pl.BlockSpec((height, width), lambda g: (0, place(g)))
    return pl.pallas_call(
        functools.partial(attend_kernel, groups),
        grid=(local_heads,),
        out_shape=jax.ShapeDtypeStruct((rows, heads * HEAD_DIM), jnp.bfloat16),
        in_specs=[
            block(rows, groups * HEAD_DIM, lambda g: g),
            block(rows, HEAD_DIM, lambda g: heads + g),
            block(rows, HEAD_DIM, lambda g: heads + local_heads + g),
            block(cached, HEAD_DIM, lambda g: g),
            block(cached, HEAD_DIM, lambda g: g),
        ],
        out_specs=block(rows, groups * HEAD_DIM, lambda g: g),
        cost_estimate=pl.CostEstimate(
            flops=4 * heads * rows * (cached + rows) * HEAD_DIM,
            bytes_accessed=4 * heads * rows * HEAD_DIM,
            transcendentals=heads * rows * (cached + rows),
        ),
        compiler_params=pltpu.CompilerParams(vmem_limit_bytes=24 << 20),
        name="attend",
    )(projected, projected, projected, cached_key, cached_value)


def project_kernel(chips, cores, n_ref, w_ref, o_ref, held, total, copy_sem, ring_send, ring_recv, pair_send, pair_recv):
    me = lax.axis_index("context")
    core = lax.rem(me, cores)
    chip = me // cores
    length = chips // 2

    def place_to_chip(place):
        side = place // length
        along = (1 - side) * place + side * (chips - 1 - place)
        return 2 * along + side

    side = lax.rem(chip, 2)
    along = chip // 2
    spot = (1 - side) * along + side * (chips - 1 - along)
    right = place_to_chip(lax.rem(spot + 1, chips)) * cores + core
    left = place_to_chip(lax.rem(spot + chips - 1, chips)) * cores + core
    sibling = chip * cores + (cores - 1 - core)
    partners = [right, left] + ([sibling] if cores == 2 else [])

    own = [
        pltpu.make_async_copy(w_ref.at[way], held.at[way, chip, core], copy_sem.at[way])
        for way in range(2)
    ]
    for copy in own:
        copy.start()
    barrier = pltpu.get_barrier_semaphore()
    for partner in partners:
        pl.semaphore_signal(
            barrier, inc=1, device_id={"context": partner}, device_id_type=pl.DeviceIdType.MESH
        )
    pl.semaphore_wait(barrier, len(partners))
    total[...] = jnp.zeros_like(total)
    for copy in own:
        copy.wait()

    def origin(way, step):
        return place_to_chip(lax.rem(spot + (chips - step if way == 0 else step), chips))

    def ring(way, step):
        piece = held.at[way, origin(way, step), core]
        return pltpu.make_async_remote_copy(
            src_ref=piece,
            dst_ref=piece,
            send_sem=ring_send.at[way, step],
            recv_sem=ring_recv.at[way, step],
            device_id={"context": right if way == 0 else left},
            device_id_type=pl.DeviceIdType.MESH,
        )

    def arrived(way, step):
        piece = held.at[way, origin(way, step), core]
        return pltpu.make_async_remote_copy(
            src_ref=piece,
            dst_ref=piece,
            send_sem=ring_send.at[way, step - 1],
            recv_sem=ring_recv.at[way, step - 1],
            device_id={"context": right if way == 0 else left},
            device_id_type=pl.DeviceIdType.MESH,
        )

    def pair(way, step, from_core):
        piece = held.at[way, origin(way, step), from_core]
        return pltpu.make_async_remote_copy(
            src_ref=piece,
            dst_ref=piece,
            send_sem=pair_send.at[way, step],
            recv_sem=pair_recv.at[way, step],
            device_id={"context": sibling},
            device_id_type=pl.DeviceIdType.MESH,
        )

    half = held.shape[4]
    depth = cores * held.shape[3]
    width = 256 if half % 256 == 0 else 128

    def compute(way, step):
        if cores == 2:
            pair(way, step, 1 - core).wait_recv()
        source = origin(way, step)

        def tile(t, carry):
            cols = pl.ds(pl.multiple_of(t * width, width), width)
            block = held[way, source, :, :, cols].reshape(depth, width)
            total[way, :, cols] += jnp.dot(n_ref[source], block, preferred_element_type=jnp.float32)
            return carry

        lax.fori_loop(0, half // width, tile, 0)

    for way in range(2):
        ring(way, 0).start()
        if cores == 2:
            pair(way, 0, core).start()

    def body(step, carry):
        for way in range(2):
            arrived(way, step).wait_recv()

            @pl.when(step < chips - 1)
            def _():
                ring(way, step).start()

            if cores == 2:
                pair(way, step, core).start()
        for way in range(2):
            compute(way, step - 1)
        return carry

    lax.fori_loop(1, chips, body, 0)
    for way in range(2):
        compute(way, chips - 1)
        for begin in range(0, half, width):
            o_ref[:, way * half + begin : way * half + begin + width] = total[
                way, :, begin : begin + width
            ].astype(o_ref.dtype)

    def drain(step, carry):
        for way in range(2):

            @pl.when(step < chips - 1)
            def _():
                ring(way, step).wait_send()

            if cores == 2:
                pair(way, step, core).wait_send()
        return carry

    lax.fori_loop(0, chips, drain, 0)


def project(normed, stacked):
    devices = lax.axis_size("context")
    cores = 2 if lax.axis_size("tensor") == 2 else 1
    chips = devices // cores
    rows = normed.shape[0]
    depth, columns = stacked.shape
    half = columns // 2
    split = jnp.stack([stacked[:, :half], stacked[:, half:]])
    return pl.pallas_call(
        functools.partial(project_kernel, chips, cores),
        out_shape=jax.ShapeDtypeStruct((rows, columns), jnp.bfloat16),
        in_specs=[
            pl.BlockSpec(memory_space=pltpu.VMEM),
            pl.BlockSpec(memory_space=pl.ANY),
        ],
        out_specs=pl.BlockSpec(memory_space=pltpu.VMEM),
        scratch_shapes=[
            pltpu.VMEM((2, chips, cores, depth, half), jnp.bfloat16),
            pltpu.VMEM((2, rows, half), jnp.float32),
            pltpu.SemaphoreType.DMA((2,)),
            pltpu.SemaphoreType.DMA((2, chips)),
            pltpu.SemaphoreType.DMA((2, chips)),
            pltpu.SemaphoreType.DMA((2, chips)),
            pltpu.SemaphoreType.DMA((2, chips)),
        ],
        compiler_params=pltpu.CompilerParams(
            collective_id=0, has_side_effects=True, vmem_limit_bytes=52 << 20
        ),
        name="project",
    )(normed.reshape(rows, chips, cores * depth).transpose(1, 0, 2), split)


def fetch_blocks(kv_cache, selected):
    local_heads = kv_cache.shape[2] // HEAD_DIM
    devices = lax.axis_size("context")
    myself = lax.axis_index("context")
    owners = selected // BLOCKS_DEV
    offsets = selected % BLOCKS_DEV
    blocks = kv_cache.reshape(BLOCKS_DEV, C_BLOCK, 2, local_heads, HEAD_DIM)
    listings = devices * PICKS
    piece_rows = C_BLOCK // devices
    flat_owner = owners.reshape(listings)
    flat_offset = offsets.reshape(listings)
    serial = jnp.arange(listings, dtype=jnp.int32)
    earlier = (flat_owner[:, None] == flat_owner[None, :]) & (serial[:, None] > serial[None, :])
    ranks = jnp.sum(earlier.astype(jnp.int32), axis=1)
    slots = jnp.arange(MOST_REQ, dtype=jnp.int32)
    hits = (flat_owner[None, :] == myself) & (ranks[None, :] == slots[:, None])
    filled = jnp.any(hits, axis=1)
    picked = jnp.sum(jnp.where(hits, flat_offset[None, :], 0), axis=1)
    outbox = jnp.where(
        filled[:, None, None, None, None],
        jnp.take(blocks, picked, axis=0),
        jnp.zeros((), jnp.bfloat16),
    )
    outbox = outbox.reshape(MOST_REQ, devices, piece_rows, 2, local_heads, HEAD_DIM)
    spread = lax.all_to_all(outbox, "context", split_axis=1, concat_axis=1, tiled=True)
    relayed = spread.reshape(MOST_REQ * devices, piece_rows, 2, local_heads, HEAD_DIM)
    forward = jnp.take(relayed, ranks * devices + flat_owner, axis=0)
    forward = forward.reshape(devices, PICKS, piece_rows, 2, local_heads, HEAD_DIM)
    collected = lax.all_to_all(forward, "context", split_axis=0, concat_axis=2, tiled=True)
    fetched = collected[0]
    cached = fetched.shape[0] * fetched.shape[1]
    cached_key = fetched[:, :, 0].reshape(cached, local_heads * HEAD_DIM)
    cached_value = fetched[:, :, 1].reshape(cached, local_heads * HEAD_DIM)
    return cached_key, cached_value


def gather_features(hidden_in):
    if lax.axis_size("tensor") != 2:
        return lax.all_gather(hidden_in, "tensor", axis=1, tiled=True)
    other = lax.ppermute(hidden_in, "tensor", [(0, 1), (1, 0)])
    first = lax.axis_index("tensor") == 0
    return jnp.concatenate(
        [jnp.where(first, hidden_in, other), jnp.where(first, other, hidden_in)], axis=1
    )


def on_device(hidden_in, norm_gain, w_query, w_key, w_value, kv_cache, selected):
    local_heads = kv_cache.shape[2] // HEAD_DIM
    groups = w_query.shape[1] // (HEAD_DIM * local_heads)
    stacked = jnp.concatenate([w_query, w_key, w_value], axis=1)
    gathered = gather_features(hidden_in)
    floats = gathered.astype(jnp.float32)
    inverse_rms = lax.rsqrt(jnp.mean(floats * floats, axis=1, keepdims=True) + 1e-05)
    normed = (floats * inverse_rms * norm_gain.astype(jnp.float32)).astype(jnp.bfloat16)
    cached_key, cached_value = fetch_blocks(kv_cache, selected)
    normed, cached_key, cached_value = lax.optimization_barrier((normed, cached_key, cached_value))
    projected = project(normed, stacked)
    return attend(projected, cached_key, cached_value, groups, local_heads)


def solution(mesh):
    return jax.shard_map(
        on_device,
        mesh=mesh,
        in_specs=(
            P("context", "tensor"),
            P(),
            P("context", "tensor"),
            P("context", "tensor"),
            P("context", "tensor"),
            P("context", None, "tensor"),
            P(),
        ),
        out_specs=P("context", "tensor"),
        check_vma=False,
    )
```

```python
import functools
import math

import jax
import jax.numpy as jnp
from jax import lax
from jax.experimental import pallas as pl
from jax.experimental.pallas import tpu as pltpu
from jax.sharding import PartitionSpec as P

HEAD_DIM = 128
C_BLOCK = 128
PICKS = 3
MOST_REQ = 6
BLOCKS_DEV = 8
ROW_TILE = 256


def attend_kernel(groups, q_ref, k_ref, v_ref, ck_ref, cv_ref, o_ref):
    rows = q_ref.shape[0]
    tile = min(ROW_TILE, rows)
    factor = math.log2(math.e) / math.sqrt(HEAD_DIM)
    dims = (((1,), (1,)), ((), ()))
    for head in range(groups):
        place = slice(head * HEAD_DIM, (head + 1) * HEAD_DIM)
        for start in range(0, rows, tile):
            stop = start + tile
            query = q_ref[start:stop, place]
            cached = lax.dot_general(query, ck_ref[...], dims, preferred_element_type=jnp.float32)
            fresh = lax.dot_general(query, k_ref[:stop, :], dims, preferred_element_type=jnp.float32)
            row = lax.broadcasted_iota(jnp.int32, fresh.shape, 0) + start
            col = lax.broadcasted_iota(jnp.int32, fresh.shape, 1)
            fresh = jnp.where(col <= row, fresh, -jnp.inf)
            top = jnp.maximum(
                jnp.max(cached, axis=1, keepdims=True), jnp.max(fresh, axis=1, keepdims=True)
            )
            cached = jnp.exp2((cached - top) * factor)
            fresh = jnp.exp2((fresh - top) * factor)
            total = jnp.sum(cached, axis=1, keepdims=True) + jnp.sum(fresh, axis=1, keepdims=True)
            inverse = 1.0 / total
            mixed = jnp.dot(
                (cached * inverse).astype(jnp.bfloat16),
                cv_ref[...],
                preferred_element_type=jnp.float32,
            )
            mixed += jnp.dot(
                (fresh * inverse).astype(jnp.bfloat16),
                v_ref[:stop, :],
                preferred_element_type=jnp.float32,
            )
            o_ref[start:stop, place] = mixed.astype(o_ref.dtype)


def attend(projected, cached_key, cached_value, groups, local_heads):
    rows = projected.shape[0]
    cached = cached_key.shape[0]
    heads = groups * local_heads
    block = lambda height, width, place: pl.BlockSpec((height, width), lambda g: (0, place(g)))
    return pl.pallas_call(
        functools.partial(attend_kernel, groups),
        grid=(local_heads,),
        out_shape=jax.ShapeDtypeStruct((rows, heads * HEAD_DIM), jnp.bfloat16),
        in_specs=[
            block(rows, groups * HEAD_DIM, lambda g: g),
            block(rows, HEAD_DIM, lambda g: heads + g),
            block(rows, HEAD_DIM, lambda g: heads + local_heads + g),
            block(cached, HEAD_DIM, lambda g: g),
            block(cached, HEAD_DIM, lambda g: g),
        ],
        out_specs=block(rows, groups * HEAD_DIM, lambda g: g),
        cost_estimate=pl.CostEstimate(
            flops=4 * heads * rows * (cached + rows) * HEAD_DIM,
            bytes_accessed=4 * heads * rows * HEAD_DIM,
            transcendentals=heads * rows * (cached + rows),
        ),
        compiler_params=pltpu.CompilerParams(vmem_limit_bytes=24 << 20),
        name="attend",
    )(projected, projected, projected, cached_key, cached_value)


def project_kernel(
    chips, cores, picks_ref, owner_ref, rank_ref, gain_ref, kv_ref, h_ref, w_ref, o_ref, f_ref,
    held, total, hidden, normed, outbox, inbox, forward, copy_sem, ring_send, ring_recv,
    pair_send, pair_recv, peer_send, peer_recv, spread_send, spread_recv, last_send, last_recv,
):
    mesh_id = pl.DeviceIdType.MESH
    me = lax.axis_index("context")
    devices = lax.axis_size("context")
    mine = lax.axis_index("tensor")
    peers = lax.axis_size("tensor")
    core = lax.rem(me, cores)
    chip = me // cores
    length = chips // 2

    def place_to_chip(place):
        side = place // length
        along = (1 - side) * place + side * (chips - 1 - place)
        return 2 * along + side

    side = lax.rem(chip, 2)
    along = chip // 2
    spot = (1 - side) * along + side * (chips - 1 - along)
    right = place_to_chip(lax.rem(spot + 1, chips)) * cores + core
    left = place_to_chip(lax.rem(spot + chips - 1, chips)) * cores + core
    sibling = chip * cores + (cores - 1 - core)

    own = [
        pltpu.make_async_copy(w_ref.at[way], held.at[way, chip, core], copy_sem.at[way])
        for way in range(2)
    ]
    own.append(pltpu.make_async_copy(h_ref, hidden.at[mine], copy_sem.at[2]))
    for copy in own:
        copy.start()
    barrier = pltpu.get_barrier_semaphore()

    def greet(k, carry):
        pl.semaphore_signal(
            barrier, inc=1, device_id={"context": lax.rem(me + k, devices)}, device_id_type=mesh_id
        )
        return carry

    lax.fori_loop(1, devices, greet, 0)
    for k in range(1, peers):
        pl.semaphore_signal(
            barrier, inc=1, device_id={"tensor": lax.rem(mine + k, peers)}, device_id_type=mesh_id
        )
    pl.semaphore_wait(barrier, devices - 1 + peers - 1)
    for copy in own:
        copy.wait()

    def origin(way, step):
        return place_to_chip(lax.rem(spot + (chips - step if way == 0 else step), chips))

    def ring(way, step, sem):
        piece = held.at[way, origin(way, step), core]
        return pltpu.make_async_remote_copy(
            src_ref=piece,
            dst_ref=piece,
            send_sem=ring_send.at[way, sem],
            recv_sem=ring_recv.at[way, sem],
            device_id={"context": right if way == 0 else left},
            device_id_type=mesh_id,
        )

    def pair(way, step, from_core):
        piece = held.at[way, origin(way, step), from_core]
        return pltpu.make_async_remote_copy(
            src_ref=piece,
            dst_ref=piece,
            send_sem=pair_send.at[way, step],
            recv_sem=pair_recv.at[way, step],
            device_id={"context": sibling},
            device_id_type=mesh_id,
        )

    def peer(k, slot):
        return pltpu.make_async_remote_copy(
            src_ref=hidden.at[slot],
            dst_ref=hidden.at[slot],
            send_sem=peer_send.at[k],
            recv_sem=peer_recv.at[k],
            device_id={"tensor": lax.rem(mine + k, peers)},
            device_id_type=mesh_id,
        )

    def spread(k, slot):
        return pltpu.make_async_remote_copy(
            src_ref=outbox.at[lax.rem(me + k, devices)],
            dst_ref=inbox.at[slot],
            send_sem=spread_send.at[k],
            recv_sem=spread_recv.at[k],
            device_id={"context": lax.rem(me + k, devices)},
            device_id_type=mesh_id,
        )

    def last(k, slot):
        return pltpu.make_async_remote_copy(
            src_ref=forward.at[lax.rem(me + k, devices)],
            dst_ref=f_ref.at[slot],
            send_sem=last_send.at[k],
            recv_sem=last_recv.at[k],
            device_id={"context": lax.rem(me + k, devices)},
            device_id_type=mesh_id,
        )

    def loop(begin, end, action):
        def run(k, carry):
            action(k)
            return carry

        lax.fori_loop(begin, end, run, 0)

    for k in range(1, peers):
        peer(k, mine).start()
    for way in range(2):
        ring(way, 0, 0).start()
        if cores == 2:
            pair(way, 0, core).start()

    def fill(slot):
        outbox[:, slot] = kv_ref[picks_ref[slot]]

    loop(0, MOST_REQ, fill)
    loop(1, devices, lambda k: spread(k, me).start())
    kept = pltpu.make_async_copy(outbox.at[me], inbox.at[me], copy_sem.at[3])
    kept.start()
    total[...] = jnp.zeros_like(total)

    half = held.shape[4]
    depth = cores * held.shape[3]
    width = 256 if half % 256 == 0 else 128

    def compute(way, step):
        if cores == 2:
            pair(way, step, 1 - core).wait_recv()
        source = origin(way, step)

        def tile(t):
            cols = pl.ds(pl.multiple_of(t * width, width), width)
            block = held[way, source, :, :, cols].reshape(depth, width)
            total[way, :, cols] += jnp.dot(normed[source], block, preferred_element_type=jnp.float32)

        loop(0, half // width, tile)

    def advance(step):
        for way in range(2):
            ring(way, step, step - 1).wait_recv()

            @pl.when(step < chips - 1)
            def _():
                ring(way, step, step).start()

            if cores == 2:
                pair(way, step, core).start()

    loop(1, length - 1, advance)
    for k in range(1, peers):
        peer(k, lax.rem(mine + peers - k, peers)).wait_recv()
    rows = hidden.shape[1]
    part = hidden.shape[2]
    height = min(64, rows)

    def normalise(t):
        at = pl.ds(pl.multiple_of(t * height, height), height)
        squares = jnp.zeros((height, 1), jnp.float32)
        for slot in range(peers):
            floats = hidden[slot, at, :].astype(jnp.float32)
            squares += jnp.sum(floats * floats, axis=1, keepdims=True)
        inverse = lax.rsqrt(squares / (peers * part) + 1e-05)
        for source in range(chips):
            slot, begin = source * depth // part, source * depth % part
            floats = hidden[slot, at, begin : begin + depth].astype(jnp.float32)
            gain = gain_ref[:, source * depth : (source + 1) * depth].astype(jnp.float32)
            normed[source, at, :] = (floats * inverse * gain).astype(jnp.bfloat16)

    loop(0, rows // height, normalise)
    advance(length - 1)
    loop(1, devices, lambda k: spread(k, lax.rem(me + devices - k, devices)).wait_recv())
    kept.wait()

    def relay(listing):
        forward[listing // PICKS, lax.rem(listing, PICKS)] = inbox[
            owner_ref[listing], rank_ref[listing]
        ]

    loop(0, devices * PICKS, relay)
    loop(1, devices, lambda k: last(k, me).start())
    kept_last = pltpu.make_async_copy(forward.at[me], f_ref.at[me], copy_sem.at[4])
    kept_last.start()

    def second(step):
        advance(step)
        for early in range(2):
            for way in range(2):
                compute(way, (step - length) * 2 + early)

    loop(length, chips, second)
    for way in range(2):
        for begin in range(0, half, width):
            o_ref[:, way * half + begin : way * half + begin + width] = total[
                way, :, begin : begin + width
            ].astype(o_ref.dtype)
    loop(1, devices, lambda k: last(k, lax.rem(me + devices - k, devices)).wait_recv())
    kept_last.wait()

    def drain(step):
        for way in range(2):

            @pl.when(step < chips - 1)
            def _():
                ring(way, step, step).wait_send()

            if cores == 2:
                pair(way, step, core).wait_send()

    loop(0, chips, drain)
    loop(1, devices, lambda k: spread(k, me).wait_send())
    loop(1, devices, lambda k: last(k, me).wait_send())
    for k in range(1, peers):
        peer(k, mine).wait_send()


def project(hidden_in, norm_gain, stacked, kv_cache, picked, owners, ranks):
    devices = lax.axis_size("context")
    peers = lax.axis_size("tensor")
    cores = 2 if peers == 2 else 1
    chips = devices // cores
    rows, part = hidden_in.shape
    depth, columns = stacked.shape
    half = columns // 2
    span = kv_cache.shape[2]
    piece = C_BLOCK // devices
    split = jnp.stack([stacked[:, :half], stacked[:, half:]])
    smem = pl.BlockSpec(memory_space=pltpu.SMEM)
    vmem = pl.BlockSpec(memory_space=pltpu.VMEM)
    anywhere = pl.BlockSpec(memory_space=pl.ANY)
    sems = lambda *shape: pltpu.SemaphoreType.DMA(shape)
    return pl.pallas_call(
        functools.partial(project_kernel, chips, cores),
        out_shape=(
            jax.ShapeDtypeStruct((rows, columns), jnp.bfloat16),
            jax.ShapeDtypeStruct((devices, PICKS, piece, 2, span), jnp.bfloat16),
        ),
        in_specs=[smem, smem, smem, vmem, vmem, anywhere, anywhere],
        out_specs=(vmem, vmem),
        scratch_shapes=[
            pltpu.VMEM((2, chips, cores, depth, half), jnp.bfloat16),
            pltpu.VMEM((2, rows, half), jnp.float32),
            pltpu.VMEM((peers, rows, part), jnp.bfloat16),
            pltpu.VMEM((chips, rows, cores * depth), jnp.bfloat16),
            pltpu.VMEM((devices, MOST_REQ, piece, 2, span), jnp.bfloat16),
            pltpu.VMEM((devices, MOST_REQ, piece, 2, span), jnp.bfloat16),
            pltpu.VMEM((devices, PICKS, piece, 2, span), jnp.bfloat16),
            sems(5),
            sems(2, chips),
            sems(2, chips),
            sems(2, chips),
            sems(2, chips),
            sems(peers),
            sems(peers),
            sems(devices),
            sems(devices),
            sems(devices),
            sems(devices),
        ],
        compiler_params=pltpu.CompilerParams(
            collective_id=0, has_side_effects=True, vmem_limit_bytes=58 << 20
        ),
        name="project",
    )(
        picked,
        owners,
        ranks,
        norm_gain.reshape(1, -1),
        kv_cache.reshape(BLOCKS_DEV, devices, piece, 2, span),
        hidden_in,
        split,
    )


def on_device(hidden_in, norm_gain, w_query, w_key, w_value, kv_cache, selected):
    local_heads = kv_cache.shape[2] // HEAD_DIM
    groups = w_query.shape[1] // (HEAD_DIM * local_heads)
    devices = lax.axis_size("context")
    stacked = jnp.concatenate([w_query, w_key, w_value], axis=1)
    owners = (selected // BLOCKS_DEV).reshape(devices * PICKS)
    offsets = (selected % BLOCKS_DEV).reshape(devices * PICKS)
    serial = jnp.arange(devices * PICKS, dtype=jnp.int32)
    earlier = (owners[:, None] == owners[None, :]) & (serial[:, None] > serial[None, :])
    ranks = jnp.sum(earlier.astype(jnp.int32), axis=1)
    slots = jnp.arange(MOST_REQ, dtype=jnp.int32)
    hits = (owners[None, :] == lax.axis_index("context")) & (ranks[None, :] == slots[:, None])
    picked = jnp.sum(jnp.where(hits, offsets[None, :], 0), axis=1)
    projected, fetched = project(hidden_in, norm_gain, stacked, kv_cache, picked, owners, ranks)
    fetched = fetched.transpose(1, 0, 2, 3, 4).reshape(PICKS * C_BLOCK, 2, kv_cache.shape[2])
    return attend(projected, fetched[:, 0], fetched[:, 1], groups, local_heads)


def solution(mesh):
    return jax.shard_map(
        on_device,
        mesh=mesh,
        in_specs=(
            P("context", "tensor"),
            P(),
            P("context", "tensor"),
            P("context", "tensor"),
            P("context", "tensor"),
            P("context", None, "tensor"),
            P(),
        ),
        out_specs=P("context", "tensor"),
        check_vma=False,
    )
```

```python
import functools
import math

import jax
import jax.numpy as jnp
from jax import lax
from jax.experimental import pallas as pl
from jax.experimental.pallas import tpu as pltpu
from jax.sharding import PartitionSpec as P

HEAD_DIM = 128
C_BLOCK = 128
PICKS = 3
MOST_REQ = 6
BLOCKS_DEV = 8
ROW_TILE = 256


def attend_kernel(groups, q_ref, k_ref, v_ref, ck_ref, cv_ref, o_ref):
    rows = q_ref.shape[0]
    tile = min(ROW_TILE, rows)
    factor = math.log2(math.e) / math.sqrt(HEAD_DIM)
    dims = (((1,), (1,)), ((), ()))
    for head in range(groups):
        place = slice(head * HEAD_DIM, (head + 1) * HEAD_DIM)
        for start in range(0, rows, tile):
            stop = start + tile
            query = q_ref[start:stop, place]
            cached = lax.dot_general(query, ck_ref[...], dims, preferred_element_type=jnp.float32)
            fresh = lax.dot_general(query, k_ref[:stop, :], dims, preferred_element_type=jnp.float32)
            row = lax.broadcasted_iota(jnp.int32, fresh.shape, 0) + start
            col = lax.broadcasted_iota(jnp.int32, fresh.shape, 1)
            fresh = jnp.where(col <= row, fresh, -jnp.inf)
            top = jnp.maximum(
                jnp.max(cached, axis=1, keepdims=True), jnp.max(fresh, axis=1, keepdims=True)
            )
            cached = jnp.exp2((cached - top) * factor)
            fresh = jnp.exp2((fresh - top) * factor)
            total = jnp.sum(cached, axis=1, keepdims=True) + jnp.sum(fresh, axis=1, keepdims=True)
            inverse = 1.0 / total
            mixed = jnp.dot(
                (cached * inverse).astype(jnp.bfloat16),
                cv_ref[...],
                preferred_element_type=jnp.float32,
            )
            mixed += jnp.dot(
                (fresh * inverse).astype(jnp.bfloat16),
                v_ref[:stop, :],
                preferred_element_type=jnp.float32,
            )
            o_ref[start:stop, place] = mixed.astype(o_ref.dtype)


def attend(projected, cached_key, cached_value, groups, local_heads):
    rows = projected.shape[0]
    cached = cached_key.shape[0]
    heads = groups * local_heads
    block = lambda height, width, place: pl.BlockSpec((height, width), lambda g: (0, place(g)))
    return pl.pallas_call(
        functools.partial(attend_kernel, groups),
        grid=(local_heads,),
        out_shape=jax.ShapeDtypeStruct((rows, heads * HEAD_DIM), jnp.bfloat16),
        in_specs=[
            block(rows, groups * HEAD_DIM, lambda g: g),
            block(rows, HEAD_DIM, lambda g: heads + g),
            block(rows, HEAD_DIM, lambda g: heads + local_heads + g),
            block(cached, HEAD_DIM, lambda g: g),
            block(cached, HEAD_DIM, lambda g: g),
        ],
        out_specs=block(rows, groups * HEAD_DIM, lambda g: g),
        cost_estimate=pl.CostEstimate(
            flops=4 * heads * rows * (cached + rows) * HEAD_DIM,
            bytes_accessed=4 * heads * rows * HEAD_DIM,
            transcendentals=heads * rows * (cached + rows),
        ),
        compiler_params=pltpu.CompilerParams(vmem_limit_bytes=24 << 20),
        name="attend",
    )(projected, projected, projected, cached_key, cached_value)


def project_kernel(
    chips, cores, picks_ref, owner_ref, rank_ref, gain_ref, kv_ref, h_ref, wq_ref, wk_ref, wv_ref, o_ref, f_ref,
    held, total, hidden, normed, outbox, inbox, forward, copy_sem, ring_send, ring_recv,
    pair_send, pair_recv, peer_send, peer_recv, spread_send, spread_recv, last_send, last_recv,
):
    mesh_id = pl.DeviceIdType.MESH
    me = lax.axis_index("context")
    devices = lax.axis_size("context")
    mine = lax.axis_index("tensor")
    peers = lax.axis_size("tensor")
    core = lax.rem(me, cores)
    chip = me // cores
    length = chips // 2

    def place_to_chip(place):
        side = place // length
        along = (1 - side) * place + side * (chips - 1 - place)
        return 2 * along + side

    side = lax.rem(chip, 2)
    along = chip // 2
    spot = (1 - side) * along + side * (chips - 1 - along)
    right = place_to_chip(lax.rem(spot + 1, chips)) * cores + core
    left = place_to_chip(lax.rem(spot + chips - 1, chips)) * cores + core
    sibling = chip * cores + (cores - 1 - core)

    half = held.shape[4]
    rest = wq_ref.shape[1] - half
    keys = wk_ref.shape[1]
    later = held.at[1, chip, core]
    own = [
        pltpu.make_async_copy(wq_ref.at[:, :half], held.at[0, chip, core], copy_sem.at[0]),
        pltpu.make_async_copy(wq_ref.at[:, half:], later.at[:, :rest], copy_sem.at[1]),
        pltpu.make_async_copy(h_ref, hidden.at[mine], copy_sem.at[2]),
        pltpu.make_async_copy(wk_ref, later.at[:, rest : rest + keys], copy_sem.at[5]),
        pltpu.make_async_copy(wv_ref, later.at[:, rest + keys :], copy_sem.at[6]),
    ]
    for copy in own:
        copy.start()
    barrier = pltpu.get_barrier_semaphore()

    def greet(k, carry):
        pl.semaphore_signal(
            barrier, inc=1, device_id={"context": lax.rem(me + k, devices)}, device_id_type=mesh_id
        )
        return carry

    lax.fori_loop(1, devices, greet, 0)
    for k in range(1, peers):
        pl.semaphore_signal(
            barrier, inc=1, device_id={"tensor": lax.rem(mine + k, peers)}, device_id_type=mesh_id
        )
    pl.semaphore_wait(barrier, devices - 1 + peers - 1)
    for copy in own:
        copy.wait()

    def origin(way, step):
        return place_to_chip(lax.rem(spot + (chips - step if way == 0 else step), chips))

    def ring(way, step, sem):
        piece = held.at[way, origin(way, step), core]
        return pltpu.make_async_remote_copy(
            src_ref=piece,
            dst_ref=piece,
            send_sem=ring_send.at[way, sem],
            recv_sem=ring_recv.at[way, sem],
            device_id={"context": right if way == 0 else left},
            device_id_type=mesh_id,
        )

    def pair(way, step, from_core):
        piece = held.at[way, origin(way, step), from_core]
        return pltpu.make_async_remote_copy(
            src_ref=piece,
            dst_ref=piece,
            send_sem=pair_send.at[way, step],
            recv_sem=pair_recv.at[way, step],
            device_id={"context": sibling},
            device_id_type=mesh_id,
        )

    def peer(k, slot):
        return pltpu.make_async_remote_copy(
            src_ref=hidden.at[slot],
            dst_ref=hidden.at[slot],
            send_sem=peer_send.at[k],
            recv_sem=peer_recv.at[k],
            device_id={"tensor": lax.rem(mine + k, peers)},
            device_id_type=mesh_id,
        )

    def spread(k, slot):
        return pltpu.make_async_remote_copy(
            src_ref=outbox.at[lax.rem(me + k, devices)],
            dst_ref=inbox.at[slot],
            send_sem=spread_send.at[k],
            recv_sem=spread_recv.at[k],
            device_id={"context": lax.rem(me + k, devices)},
            device_id_type=mesh_id,
        )

    def last(k, slot):
        return pltpu.make_async_remote_copy(
            src_ref=forward.at[lax.rem(me + k, devices)],
            dst_ref=f_ref.at[slot],
            send_sem=last_send.at[k],
            recv_sem=last_recv.at[k],
            device_id={"context": lax.rem(me + k, devices)},
            device_id_type=mesh_id,
        )

    def loop(begin, end, action):
        def run(k, carry):
            action(k)
            return carry

        lax.fori_loop(begin, end, run, 0)

    for k in range(1, peers):
        peer(k, mine).start()
    for way in range(2):
        ring(way, 0, 0).start()
        if cores == 2:
            pair(way, 0, core).start()

    def fill(slot):
        outbox[:, slot] = kv_ref[picks_ref[slot]]

    loop(0, MOST_REQ, fill)
    loop(1, devices, lambda k: spread(k, me).start())
    kept = pltpu.make_async_copy(outbox.at[me], inbox.at[me], copy_sem.at[3])
    kept.start()
    total[...] = jnp.zeros_like(total)

    depth = cores * held.shape[3]
    width = 256 if half % 256 == 0 else 128

    def compute(way, step):
        if cores == 2:
            pair(way, step, 1 - core).wait_recv()
        source = origin(way, step)

        def tile(t):
            cols = pl.ds(pl.multiple_of(t * width, width), width)
            block = held[way, source, :, :, cols].reshape(depth, width)
            total[way, :, cols] += jnp.dot(normed[source], block, preferred_element_type=jnp.float32)

        loop(0, half // width, tile)

    def advance(step):
        for way in range(2):
            ring(way, step, step - 1).wait_recv()

            @pl.when(step < chips - 1)
            def _():
                ring(way, step, step).start()

            if cores == 2:
                pair(way, step, core).start()

    loop(1, length, advance)
    for k in range(1, peers):
        peer(k, lax.rem(mine + peers - k, peers)).wait_recv()
    rows = hidden.shape[1]
    part = hidden.shape[2]
    height = min(64, rows)

    def normalise(t):
        at = pl.ds(pl.multiple_of(t * height, height), height)
        squares = jnp.zeros((height, 1), jnp.float32)
        for slot in range(peers):
            floats = hidden[slot, at, :].astype(jnp.float32)
            squares += jnp.sum(floats * floats, axis=1, keepdims=True)
        inverse = lax.rsqrt(squares / (peers * part) + 1e-05)
        for source in range(chips):
            slot, begin = source * depth // part, source * depth % part
            floats = hidden[slot, at, begin : begin + depth].astype(jnp.float32)
            gain = gain_ref[:, source * depth : (source + 1) * depth].astype(jnp.float32)
            normed[source, at, :] = (floats * inverse * gain).astype(jnp.bfloat16)

    loop(0, rows // height, normalise)
    advance(length)
    loop(1, devices, lambda k: spread(k, lax.rem(me + devices - k, devices)).wait_recv())
    kept.wait()

    def relay(listing):
        forward[listing // PICKS, lax.rem(listing, PICKS)] = inbox[
            owner_ref[listing], rank_ref[listing]
        ]

    loop(0, devices * PICKS, relay)
    loop(1, devices, lambda k: last(k, me).start())
    kept_last = pltpu.make_async_copy(forward.at[me], f_ref.at[me], copy_sem.at[4])
    kept_last.start()

    def second(step):
        advance(step)
        for early in range(2):
            for way in range(2):
                compute(way, (step - length - 1) * 2 + early)

    loop(length + 1, chips, second)
    for way in range(2):
        compute(way, chips - 2)
    for way in range(2):
        compute(way, chips - 1)
        for begin in range(0, half, width):
            o_ref[:, way * half + begin : way * half + begin + width] = total[
                way, :, begin : begin + width
            ].astype(o_ref.dtype)
    loop(1, devices, lambda k: last(k, lax.rem(me + devices - k, devices)).wait_recv())
    kept_last.wait()

    def drain(step):
        for way in range(2):

            @pl.when(step < chips - 1)
            def _():
                ring(way, step, step).wait_send()

            if cores == 2:
                pair(way, step, core).wait_send()

    loop(0, chips, drain)
    loop(1, devices, lambda k: spread(k, me).wait_send())
    loop(1, devices, lambda k: last(k, me).wait_send())
    for k in range(1, peers):
        peer(k, mine).wait_send()


def project(hidden_in, norm_gain, weights, kv_cache, picked, owners, ranks):
    devices = lax.axis_size("context")
    peers = lax.axis_size("tensor")
    cores = 2 if peers == 2 else 1
    chips = devices // cores
    rows, part = hidden_in.shape
    depth = weights[0].shape[0]
    columns = sum(weight.shape[1] for weight in weights)
    half = columns // 2
    span = kv_cache.shape[2]
    piece = C_BLOCK // devices
    smem = pl.BlockSpec(memory_space=pltpu.SMEM)
    vmem = pl.BlockSpec(memory_space=pltpu.VMEM)
    anywhere = pl.BlockSpec(memory_space=pl.ANY)
    sems = lambda *shape: pltpu.SemaphoreType.DMA(shape)
    return pl.pallas_call(
        functools.partial(project_kernel, chips, cores),
        out_shape=(
            jax.ShapeDtypeStruct((rows, columns), jnp.bfloat16),
            jax.ShapeDtypeStruct((devices, PICKS, piece, 2, span), jnp.bfloat16),
        ),
        in_specs=[smem, smem, smem, vmem, vmem, anywhere, anywhere, anywhere, anywhere],
        out_specs=(vmem, vmem),
        scratch_shapes=[
            pltpu.VMEM((2, chips, cores, depth, half), jnp.bfloat16),
            pltpu.VMEM((2, rows, half), jnp.float32),
            pltpu.VMEM((peers, rows, part), jnp.bfloat16),
            pltpu.VMEM((chips, rows, cores * depth), jnp.bfloat16),
            pltpu.VMEM((devices, MOST_REQ, piece, 2, span), jnp.bfloat16),
            pltpu.VMEM((devices, MOST_REQ, piece, 2, span), jnp.bfloat16),
            pltpu.VMEM((devices, PICKS, piece, 2, span), jnp.bfloat16),
            sems(7),
            sems(2, chips),
            sems(2, chips),
            sems(2, chips),
            sems(2, chips),
            sems(peers),
            sems(peers),
            sems(devices),
            sems(devices),
            sems(devices),
            sems(devices),
        ],
        compiler_params=pltpu.CompilerParams(
            collective_id=0, has_side_effects=True, vmem_limit_bytes=58 << 20
        ),
        name="project",
    )(
        picked,
        owners,
        ranks,
        norm_gain.reshape(1, -1),
        kv_cache.reshape(BLOCKS_DEV, devices, piece, 2, span),
        hidden_in,
        *weights,
    )


def on_device(hidden_in, norm_gain, w_query, w_key, w_value, kv_cache, selected):
    local_heads = kv_cache.shape[2] // HEAD_DIM
    groups = w_query.shape[1] // (HEAD_DIM * local_heads)
    devices = lax.axis_size("context")
    weights = (w_query, w_key, w_value)
    owners = (selected // BLOCKS_DEV).reshape(devices * PICKS)
    offsets = (selected % BLOCKS_DEV).reshape(devices * PICKS)
    serial = jnp.arange(devices * PICKS, dtype=jnp.int32)
    earlier = (owners[:, None] == owners[None, :]) & (serial[:, None] > serial[None, :])
    ranks = jnp.sum(earlier.astype(jnp.int32), axis=1)
    slots = jnp.arange(MOST_REQ, dtype=jnp.int32)
    hits = (owners[None, :] == lax.axis_index("context")) & (ranks[None, :] == slots[:, None])
    picked = jnp.sum(jnp.where(hits, offsets[None, :], 0), axis=1)
    projected, fetched = project(hidden_in, norm_gain, weights, kv_cache, picked, owners, ranks)
    fetched = fetched.transpose(1, 0, 2, 3, 4).reshape(PICKS * C_BLOCK, 2, kv_cache.shape[2])
    return attend(projected, fetched[:, 0], fetched[:, 1], groups, local_heads)


def solution(mesh):
    return jax.shard_map(
        on_device,
        mesh=mesh,
        in_specs=(
            P("context", "tensor"),
            P(),
            P("context", "tensor"),
            P("context", "tensor"),
            P("context", "tensor"),
            P("context", None, "tensor"),
            P(),
        ),
        out_specs=P("context", "tensor"),
        check_vma=False,
    )
```

```python
import functools
import math

import jax
import jax.numpy as jnp
from jax import lax
from jax.experimental import pallas as pl
from jax.experimental.pallas import tpu as pltpu
from jax.sharding import PartitionSpec as P

HEAD_DIM = 128
C_BLOCK = 128
PICKS = 3
MOST_REQ = 6
BLOCKS_DEV = 8
ROW_TILE = 256


def attend_kernel(groups, q_ref, k_ref, v_ref, ck_ref, cv_ref, o_ref):
    rows = q_ref.shape[0]
    tile = min(ROW_TILE, rows)
    factor = math.log2(math.e) / math.sqrt(HEAD_DIM)
    dims = (((1,), (1,)), ((), ()))
    for head in range(groups):
        place = slice(head * HEAD_DIM, (head + 1) * HEAD_DIM)
        for start in range(0, rows, tile):
            stop = start + tile
            query = q_ref[start:stop, place]
            cached = lax.dot_general(query, ck_ref[...], dims, preferred_element_type=jnp.float32)
            fresh = lax.dot_general(query, k_ref[:stop, :], dims, preferred_element_type=jnp.float32)
            row = lax.broadcasted_iota(jnp.int32, fresh.shape, 0) + start
            col = lax.broadcasted_iota(jnp.int32, fresh.shape, 1)
            fresh = jnp.where(col <= row, fresh, -jnp.inf)
            top = jnp.maximum(
                jnp.max(cached, axis=1, keepdims=True), jnp.max(fresh, axis=1, keepdims=True)
            )
            cached = jnp.exp2((cached - top) * factor)
            fresh = jnp.exp2((fresh - top) * factor)
            total = jnp.sum(cached, axis=1, keepdims=True) + jnp.sum(fresh, axis=1, keepdims=True)
            inverse = 1.0 / total
            mixed = jnp.dot(
                (cached * inverse).astype(jnp.bfloat16),
                cv_ref[...],
                preferred_element_type=jnp.float32,
            )
            mixed += jnp.dot(
                (fresh * inverse).astype(jnp.bfloat16),
                v_ref[:stop, :],
                preferred_element_type=jnp.float32,
            )
            o_ref[start:stop, place] = mixed.astype(o_ref.dtype)


def attend(projected, cached_key, cached_value, groups, local_heads):
    rows = projected.shape[0]
    cached = cached_key.shape[0]
    heads = groups * local_heads
    block = lambda height, width, place: pl.BlockSpec((height, width), lambda g: (0, place(g)))
    return pl.pallas_call(
        functools.partial(attend_kernel, groups),
        grid=(local_heads,),
        out_shape=jax.ShapeDtypeStruct((rows, heads * HEAD_DIM), jnp.bfloat16),
        in_specs=[
            block(rows, groups * HEAD_DIM, lambda g: g),
            block(rows, HEAD_DIM, lambda g: heads + g),
            block(rows, HEAD_DIM, lambda g: heads + local_heads + g),
            block(cached, HEAD_DIM, lambda g: g),
            block(cached, HEAD_DIM, lambda g: g),
        ],
        out_specs=block(rows, groups * HEAD_DIM, lambda g: g),
        cost_estimate=pl.CostEstimate(
            flops=4 * heads * rows * (cached + rows) * HEAD_DIM,
            bytes_accessed=4 * heads * rows * HEAD_DIM,
            transcendentals=heads * rows * (cached + rows),
        ),
        compiler_params=pltpu.CompilerParams(vmem_limit_bytes=24 << 20),
        name="attend",
    )(projected, projected, projected, cached_key, cached_value)


def project_kernel(
    chips, cores, picks_ref, owner_ref, rank_ref, gain_ref, kv_ref, h_ref, wq_ref, wk_ref, wv_ref, o_ref, f_ref,
    held, total, hidden, normed, outbox, inbox, forward, copy_sem, ring_send, ring_recv,
    pair_send, pair_recv, peer_send, peer_recv, spread_send, spread_recv, last_send, last_recv,
):
    mesh_id = pl.DeviceIdType.MESH
    me = lax.axis_index("context")
    devices = lax.axis_size("context")
    mine = lax.axis_index("tensor")
    peers = lax.axis_size("tensor")
    core = lax.rem(me, cores)
    chip = me // cores
    length = chips // 2

    def place_to_chip(place):
        side = place // length
        along = (1 - side) * place + side * (chips - 1 - place)
        return 2 * along + side

    side = lax.rem(chip, 2)
    along = chip // 2
    spot = (1 - side) * along + side * (chips - 1 - along)
    right = place_to_chip(lax.rem(spot + 1, chips)) * cores + core
    left = place_to_chip(lax.rem(spot + chips - 1, chips)) * cores + core
    sibling = chip * cores + (cores - 1 - core)

    half = held.shape[4]
    rest = wq_ref.shape[1] - half
    keys = wk_ref.shape[1]
    later = held.at[1, chip, core]
    own = [
        pltpu.make_async_copy(wq_ref.at[:, :half], held.at[0, chip, core], copy_sem.at[0]),
        pltpu.make_async_copy(wq_ref.at[:, half:], later.at[:, :rest], copy_sem.at[1]),
        pltpu.make_async_copy(h_ref, hidden.at[mine], copy_sem.at[2]),
        pltpu.make_async_copy(wk_ref, later.at[:, rest : rest + keys], copy_sem.at[5]),
        pltpu.make_async_copy(wv_ref, later.at[:, rest + keys :], copy_sem.at[6]),
    ]
    for copy in own:
        copy.start()
    barrier = pltpu.get_barrier_semaphore()

    def greet(k, carry):
        pl.semaphore_signal(
            barrier, inc=1, device_id={"context": lax.rem(me + k, devices)}, device_id_type=mesh_id
        )
        return carry

    lax.fori_loop(1, devices, greet, 0)
    for k in range(1, peers):
        pl.semaphore_signal(
            barrier, inc=1, device_id={"tensor": lax.rem(mine + k, peers)}, device_id_type=mesh_id
        )
    pl.semaphore_wait(barrier, devices - 1 + peers - 1)
    for copy in own:
        copy.wait()

    def origin(way, step):
        return place_to_chip(lax.rem(spot + (chips - step if way == 0 else step), chips))

    def ring(way, step, sem):
        piece = held.at[way, origin(way, step), core]
        return pltpu.make_async_remote_copy(
            src_ref=piece,
            dst_ref=piece,
            send_sem=ring_send.at[way, sem],
            recv_sem=ring_recv.at[way, sem],
            device_id={"context": right if way == 0 else left},
            device_id_type=mesh_id,
        )

    def pair(way, step, from_core):
        piece = held.at[way, origin(way, step), from_core]
        return pltpu.make_async_remote_copy(
            src_ref=piece,
            dst_ref=piece,
            send_sem=pair_send.at[way, step],
            recv_sem=pair_recv.at[way, step],
            device_id={"context": sibling},
            device_id_type=mesh_id,
        )

    def peer(k, slot):
        return pltpu.make_async_remote_copy(
            src_ref=hidden.at[slot],
            dst_ref=hidden.at[slot],
            send_sem=peer_send.at[k],
            recv_sem=peer_recv.at[k],
            device_id={"tensor": lax.rem(mine + k, peers)},
            device_id_type=mesh_id,
        )

    def spread(k, slot):
        return pltpu.make_async_remote_copy(
            src_ref=outbox.at[lax.rem(me + k, devices)],
            dst_ref=inbox.at[slot],
            send_sem=spread_send.at[k],
            recv_sem=spread_recv.at[k],
            device_id={"context": lax.rem(me + k, devices)},
            device_id_type=mesh_id,
        )

    def last(k, slot):
        return pltpu.make_async_remote_copy(
            src_ref=forward.at[lax.rem(me + k, devices)],
            dst_ref=f_ref.at[slot],
            send_sem=last_send.at[k],
            recv_sem=last_recv.at[k],
            device_id={"context": lax.rem(me + k, devices)},
            device_id_type=mesh_id,
        )

    def loop(begin, end, action):
        def run(k, carry):
            action(k)
            return carry

        lax.fori_loop(begin, end, run, 0)

    for k in range(1, peers):
        peer(k, mine).start()
    for way in range(2):
        ring(way, 0, 0).start()
        if cores == 2:
            pair(way, 0, core).start()

    def fill(slot):
        outbox[:, slot] = kv_ref[picks_ref[slot]]

    loop(0, MOST_REQ, fill)
    loop(1, devices, lambda k: spread(k, me).start())
    kept = pltpu.make_async_copy(outbox.at[me], inbox.at[me], copy_sem.at[3])
    kept.start()
    total[...] = jnp.zeros_like(total)

    depth = cores * held.shape[3]
    width = 256 if half % 256 == 0 else 128

    def compute(way, step):
        if cores == 2:
            pair(way, step, 1 - core).wait_recv()
        source = origin(way, step)

        def tile(t):
            cols = pl.ds(pl.multiple_of(t * width, width), width)
            block = held[way, source, :, :, cols].reshape(depth, width)
            total[way, :, cols] += jnp.dot(normed[source], block, preferred_element_type=jnp.float32)

        loop(0, half // width, tile)

    def advance(step):
        for way in range(2):
            ring(way, step, step - 1).wait_recv()

            @pl.when(step < chips - 1)
            def _():
                ring(way, step, step).start()

            if cores == 2:
                pair(way, step, core).start()

    loop(1, length - 1, advance)
    for k in range(1, peers):
        peer(k, lax.rem(mine + peers - k, peers)).wait_recv()
    rows = hidden.shape[1]
    part = hidden.shape[2]
    height = min(64, rows)

    def normalise(t):
        at = pl.ds(pl.multiple_of(t * height, height), height)
        squares = jnp.zeros((height, 1), jnp.float32)
        for slot in range(peers):
            floats = hidden[slot, at, :].astype(jnp.float32)
            squares += jnp.sum(floats * floats, axis=1, keepdims=True)
        inverse = lax.rsqrt(squares / (peers * part) + 1e-05)
        for source in range(chips):
            slot, begin = source * depth // part, source * depth % part
            floats = hidden[slot, at, begin : begin + depth].astype(jnp.float32)
            gain = gain_ref[:, source * depth : (source + 1) * depth].astype(jnp.float32)
            normed[source, at, :] = (floats * inverse * gain).astype(jnp.bfloat16)

    loop(0, rows // height, normalise)
    advance(length - 1)
    loop(1, devices, lambda k: spread(k, lax.rem(me + devices - k, devices)).wait_recv())
    kept.wait()

    def relay(listing):
        forward[listing // PICKS, lax.rem(listing, PICKS)] = inbox[
            owner_ref[listing], rank_ref[listing]
        ]

    loop(0, devices * PICKS, relay)
    loop(1, devices, lambda k: last(k, me).start())
    kept_last = pltpu.make_async_copy(forward.at[me], f_ref.at[me], copy_sem.at[4])
    kept_last.start()

    def second(step):
        advance(step)
        for early in range(2):
            for way in range(2):
                compute(way, (step - length) * 2 + early)

    loop(length, chips, second)
    for way in range(2):
        for begin in range(0, half, width):
            o_ref[:, way * half + begin : way * half + begin + width] = total[
                way, :, begin : begin + width
            ].astype(o_ref.dtype)
    loop(1, devices, lambda k: last(k, lax.rem(me + devices - k, devices)).wait_recv())
    kept_last.wait()

    def drain(step):
        for way in range(2):

            @pl.when(step < chips - 1)
            def _():
                ring(way, step, step).wait_send()

            if cores == 2:
                pair(way, step, core).wait_send()

    loop(0, chips, drain)
    loop(1, devices, lambda k: spread(k, me).wait_send())
    loop(1, devices, lambda k: last(k, me).wait_send())
    for k in range(1, peers):
        peer(k, mine).wait_send()


def project(hidden_in, norm_gain, weights, kv_cache, picked, owners, ranks):
    devices = lax.axis_size("context")
    peers = lax.axis_size("tensor")
    cores = 2 if peers == 2 else 1
    chips = devices // cores
    rows, part = hidden_in.shape
    depth = weights[0].shape[0]
    columns = sum(weight.shape[1] for weight in weights)
    half = columns // 2
    span = kv_cache.shape[2]
    piece = C_BLOCK // devices
    smem = pl.BlockSpec(memory_space=pltpu.SMEM)
    vmem = pl.BlockSpec(memory_space=pltpu.VMEM)
    anywhere = pl.BlockSpec(memory_space=pl.ANY)
    sems = lambda *shape: pltpu.SemaphoreType.DMA(shape)
    return pl.pallas_call(
        functools.partial(project_kernel, chips, cores),
        out_shape=(
            jax.ShapeDtypeStruct((rows, columns), jnp.bfloat16),
            jax.ShapeDtypeStruct((devices, PICKS, piece, 2, span), jnp.bfloat16),
        ),
        in_specs=[smem, smem, smem, vmem, vmem, anywhere, anywhere, anywhere, anywhere],
        out_specs=(vmem, vmem),
        scratch_shapes=[
            pltpu.VMEM((2, chips, cores, depth, half), jnp.bfloat16),
            pltpu.VMEM((2, rows, half), jnp.float32),
            pltpu.VMEM((peers, rows, part), jnp.bfloat16),
            pltpu.VMEM((chips, rows, cores * depth), jnp.bfloat16),
            pltpu.VMEM((devices, MOST_REQ, piece, 2, span), jnp.bfloat16),
            pltpu.VMEM((devices, MOST_REQ, piece, 2, span), jnp.bfloat16),
            pltpu.VMEM((devices, PICKS, piece, 2, span), jnp.bfloat16),
            sems(7),
            sems(2, chips),
            sems(2, chips),
            sems(2, chips),
            sems(2, chips),
            sems(peers),
            sems(peers),
            sems(devices),
            sems(devices),
            sems(devices),
            sems(devices),
        ],
        compiler_params=pltpu.CompilerParams(
            collective_id=0, has_side_effects=True, vmem_limit_bytes=58 << 20
        ),
        name="project",
    )(
        picked,
        owners,
        ranks,
        norm_gain.reshape(1, -1),
        kv_cache.reshape(BLOCKS_DEV, devices, piece, 2, span),
        hidden_in,
        *weights,
    )


def on_device(hidden_in, norm_gain, w_query, w_key, w_value, kv_cache, selected):
    local_heads = kv_cache.shape[2] // HEAD_DIM
    groups = w_query.shape[1] // (HEAD_DIM * local_heads)
    devices = lax.axis_size("context")
    weights = (w_query, w_key, w_value)
    owners = (selected // BLOCKS_DEV).reshape(devices * PICKS)
    offsets = (selected % BLOCKS_DEV).reshape(devices * PICKS)
    serial = jnp.arange(devices * PICKS, dtype=jnp.int32)
    earlier = (owners[:, None] == owners[None, :]) & (serial[:, None] > serial[None, :])
    ranks = jnp.sum(earlier.astype(jnp.int32), axis=1)
    slots = jnp.arange(MOST_REQ, dtype=jnp.int32)
    hits = (owners[None, :] == lax.axis_index("context")) & (ranks[None, :] == slots[:, None])
    picked = jnp.sum(jnp.where(hits, offsets[None, :], 0), axis=1)
    projected, fetched = project(hidden_in, norm_gain, weights, kv_cache, picked, owners, ranks)
    fetched = fetched.transpose(1, 0, 2, 3, 4).reshape(PICKS * C_BLOCK, 2, kv_cache.shape[2])
    return attend(projected, fetched[:, 0], fetched[:, 1], groups, local_heads)


def solution(mesh):
    return jax.shard_map(
        on_device,
        mesh=mesh,
        in_specs=(
            P("context", "tensor"),
            P(),
            P("context", "tensor"),
            P("context", "tensor"),
            P("context", "tensor"),
            P("context", None, "tensor"),
            P(),
        ),
        out_specs=P("context", "tensor"),
        check_vma=False,
    )
```
